256 devices in a mesh: leaf: 256 (over y, z, x, core).
Axes of the slice: x: 4, y: 4, z: 8, core: 2. Of those that a mesh axis runs over, the one named last changes fastest.
Arguments:
- fields: bfloat16 [524288, 128], P('leaf'), may hold values from -6 to 6
- in_basis: bfloat16 [524288, 128], P('leaf'), may hold values from -0.375 to 0.375
- out_basis: bfloat16 [524288, 128], P('leaf'), may hold values from -0.5 to 0.5
- couplings: bfloat16 [11, 2048, 2, 128, 128], P(None, 'leaf'), may hold values from -0.375 to 0.375
- near_blocks: bfloat16 [2048, 3, 256, 256], P('leaf'), may hold values from -0.21875 to 0.21875
Outputs:
- scattered: bfloat16 [524288, 128], P('leaf')
The draws below stay inside these ranges and needn't reach their ends.
All inputs are finite; a program needn't handle non-finite values.
Results may differ from the reference program's by a relative error of at most 0.015.
Values may be sent and summed in bfloat16 or wider, within the bound.
A program may use at most 64 MiB of HBM per device.

```python
import jax
import jax.numpy as jnp

RANK = 128
LEAF_ROWS = 256
RHS_COLS = 128
LEVELS = 11
LEAVES = 2048
NROWS = 524288


def levels(own_key, extent, cuts, low, high):
    gain = 1.0
    for dim, parts in cuts:
        draws = jax.random.uniform(jax.random.fold_in(jax.random.fold_in(own_key, 6), dim), (parts,), jnp.float32, low / len(cuts), high / len(cuts))
        gain = gain * jnp.repeat(jnp.exp(draws), extent[dim] // parts).reshape((-1,) + (1,) * (len(extent) - 1 - dim))
    return gain


def noise(stream_key, extent, spread, bound, split=(), kind=jnp.bfloat16):
    drawn = spread * jax.random.normal(stream_key, extent, jnp.float32)
    if split:
        drawn = drawn * levels(stream_key, extent, split, -0.22, 0.18)
    return jnp.clip(drawn, -bound, bound).astype(kind)


def setup_inputs(seed: int = 0) -> dict:
    keys = jax.random.split(jax.random.key(seed), 6)
    fields = noise(keys[0], (NROWS, RHS_COLS), 1.0, 6.0, ((0, 256),))
    in_basis = noise(keys[1], (NROWS, RANK), LEAF_ROWS ** -0.5, 0.375, ((0, 256),))
    out_basis = noise(keys[2], (NROWS, RANK), RANK ** -0.5, 0.5, ((0, 256),))
    couplings = noise(keys[3], (LEVELS, LEAVES, 2, RANK, RANK), (2 * RANK) ** -0.5, 0.375, ((1, 256),))
    near_blocks = noise(keys[4], (LEAVES, 3, LEAF_ROWS, LEAF_ROWS), (3 * LEAF_ROWS) ** -0.5, 0.21875, ((0, 256),))
    return {"fields": fields, "in_basis": in_basis, "out_basis": out_basis, "couplings": couplings, "near_blocks": near_blocks}


def butterfly_level(coeffs, mixing, bit_pos):
    stride = 2 ** bit_pos
    grouped = coeffs.reshape(LEAVES // (2 * stride), 2, stride, RANK, RHS_COLS)
    low_half = jnp.broadcast_to(grouped[:, 0:1], grouped.shape).reshape(coeffs.shape)
    high_half = jnp.broadcast_to(grouped[:, 1:2], grouped.shape).reshape(coeffs.shape)
    summed = jnp.einsum("bij,bjc->bic", mixing[:, 0].astype(jnp.float32), low_half.astype(jnp.float32))
    summed = summed + jnp.einsum("bij,bjc->bic", mixing[:, 1].astype(jnp.float32), high_half.astype(jnp.float32))
    return summed.astype(jnp.bfloat16)


def reference(fields, in_basis, out_basis, couplings, near_blocks):
    blocks = fields.reshape(LEAVES, LEAF_ROWS, RHS_COLS)
    basis_in = in_basis.reshape(LEAVES, LEAF_ROWS, RANK)
    coeffs = jnp.einsum("bmr,bmc->brc", basis_in.astype(jnp.float32), blocks.astype(jnp.float32)).astype(jnp.bfloat16)
    for bit_pos in range(LEVELS):
        coeffs = butterfly_level(coeffs, couplings[bit_pos], bit_pos)
    basis_out = out_basis.reshape(LEAVES, LEAF_ROWS, RANK)
    summed = jnp.einsum("bmr,brc->bmc", basis_out.astype(jnp.float32), coeffs.astype(jnp.float32))
    border = jnp.zeros((1, LEAF_ROWS, RHS_COLS), jnp.bfloat16)
    padded = jnp.concatenate([border, blocks, border], axis=0)
    for offset in range(3):
        summed = summed + jnp.einsum("bmn,bnc->bmc", near_blocks[:, offset].astype(jnp.float32), padded[offset:offset + LEAVES].astype(jnp.float32))
    return summed.reshape(NROWS, RHS_COLS).astype(jnp.bfloat16)
```

```python
import functools

import jax
import jax.numpy as jnp
from jax import lax
from jax.experimental import pallas as pl
from jax.experimental.pallas import tpu as pltpu
from jax.sharding import PartitionSpec as P

MESH = pl.DeviceIdType.MESH
F32 = jnp.float32
BF16 = jnp.bfloat16


def event_order(leaves, dev_bits):
    cost = [
        (0.9, 0.10, "c"),
        (1.7, 0.70, "x"),
        (2.4, 0.70, "x"),
        (1.7, 0.35, "z"),
        (2.4, 1.40, "z"),
        (4.0, 1.40, "z"),
        (1.7, 0.70, "y"),
        (2.4, 0.70, "y"),
    ]
    cost = [cost[level % len(cost)] for level in range(dev_bits)]
    busy = {}
    core = 0.0
    queue = []
    for leaf in range(leaves):
        core += 0.15
        start = max(core, busy.get(cost[0][2], 0.0))
        busy[cost[0][2]] = start + cost[0][1]
        queue.append((start + cost[0][1] + cost[0][0], 0, leaf))
    order = []
    while queue:
        queue.sort()
        ready, level, leaf = queue.pop(0)
        order.append((max(ready, core), level, leaf))
        core = max(ready, core) + 0.15
        if level + 1 < dev_bits:
            flight, wire, row = cost[level + 1]
            start = max(core, busy.get(row, 0.0))
            busy[row] = start + wire
            queue.append((start + wire + flight, level + 1, leaf))
    return order


def kernel(
    count,
    fields_hbm,
    in_hbm,
    out_hbm,
    coup_hbm,
    near_hbm,
    result_hbm,
    fields,
    basis_in,
    basis_out,
    coup,
    near,
    local,
    cross,
    final,
    summed,
    result,
    load_sem,
    coup_sem,
    near_sem,
    basis_sem,
    store_sem,
    halo_send,
    halo_recv,
    send_sem,
    recv_sem,
):
    leaves = near.shape[0]
    rows = near.shape[2]
    rank = basis_in.shape[1]
    levels = coup.shape[0]
    dev_bits = cross.shape[0]
    local_bits = levels - dev_bits
    me = lax.axis_index("leaf")
    right = lax.rem(me + 1, count)
    left = lax.rem(me + count - 1, count)
    sides = [lax.rem(lax.div(me, 1 << k), 2) for k in range(dev_bits)]
    partners = [me + (1 << k) * (1 - 2 * sides[k]) for k in range(dev_bits)]

    pair_rows = 2 * rows
    loads = []
    for pair in range(leaves // 2):
        at = pl.ds(pair * pair_rows, pair_rows)
        to = pl.ds(rows + pair * pair_rows, pair_rows)
        loads.append(
            (
                pltpu.make_async_copy(fields_hbm.at[at], fields.at[to], load_sem.at[0, pair]),
                pltpu.make_async_copy(in_hbm.at[at], basis_in.at[at], load_sem.at[1, pair]),
            )
        )
    coup_loads = [
        pltpu.make_async_copy(coup_hbm.at[q], coup.at[q], coup_sem.at[q]) for q in range(levels)
    ]
    near_loads = [
        pltpu.make_async_copy(near_hbm.at[b], near.at[b], near_sem.at[b]) for b in range(leaves)
    ]
    basis_load = pltpu.make_async_copy(out_hbm, basis_out, basis_sem)

    for pair in loads:
        for load in pair:
            load.start()
    for q in range(local_bits):
        coup_loads[q].start()

    barrier = pltpu.get_barrier_semaphore()
    for other in partners + [left, right]:
        pl.semaphore_signal(barrier, inc=1, device_id=(other,), device_id_type=MESH)

    for b in range(leaves):
        if b % 2 == 0:
            for load in loads[b // 2]:
                load.wait()
        local[0, b] = lax.dot_general(
            basis_in[pl.ds(b * rows, rows), :],
            fields[pl.ds((b + 1) * rows, rows), :],
            (((0,), (0,)), ((), ())),
            preferred_element_type=F32,
        ).astype(BF16)

    for q in range(local_bits, levels):
        coup_loads[q].start()
    for b in range(leaves):
        near_loads[b].start()
    basis_load.start()

    def mix(q, b, stacked):
        both = jnp.concatenate([coup[q, b, 0], coup[q, b, 1]], axis=1)
        return jnp.dot(both, stacked, preferred_element_type=F32).astype(BF16)

    copies = {}

    def send(level, b):
        copy = pltpu.make_async_remote_copy(
            src_ref=cross.at[level, b, sides[level]],
            dst_ref=cross.at[level, b, sides[level]],
            send_sem=send_sem.at[level, b],
            recv_sem=recv_sem.at[level, b],
            device_id=(partners[level],),
            device_id_type=MESH,
        )
        copy.start()
        copies[level, b] = copy

    for q in range(local_bits):
        coup_loads[q].wait()
        if q == local_bits - 1:
            pl.semaphore_wait(barrier, dev_bits + 2)
        stride = 1 << q
        for lo in range(leaves):
            if lo & stride:
                continue
            hi = lo | stride
            stacked = jnp.concatenate([local[q, lo], local[q, hi]], axis=0)
            for b in (lo, hi):
                mixed = mix(q, b, stacked)
                if q + 1 < local_bits:
                    local[q + 1, b] = mixed
                else:
                    cross[0, b, sides[0]] = mixed
                    send(0, b)

    to_left = pltpu.make_async_remote_copy(
        src_ref=fields.at[pl.ds(rows, rows)],
        dst_ref=fields.at[pl.ds((leaves + 1) * rows, rows)],
        send_sem=halo_send.at[0],
        recv_sem=halo_recv.at[0],
        device_id=(left,),
        device_id_type=MESH,
    )
    to_right = pltpu.make_async_remote_copy(
        src_ref=fields.at[pl.ds(leaves * rows, rows)],
        dst_ref=fields.at[pl.ds(0, rows)],
        send_sem=halo_send.at[1],
        recv_sem=halo_recv.at[1],
        device_id=(right,),
        device_id_type=MESH,
    )
    to_left.start()
    to_right.start()

    def near_field(b):
        near_loads[b].wait()
        if b == 0:
            to_right.wait_recv()
        if b == leaves - 1:
            to_left.wait_recv()
        total = None
        for j in range(3):
            block = fields[pl.ds((b + j) * rows, rows), :]
            if b == 0 and j == 0:
                block = jnp.where(me > 0, block, jnp.zeros_like(block))
            if b == leaves - 1 and j == 2:
                block = jnp.where(me < count - 1, block, jnp.zeros_like(block))
            term = jnp.dot(near[b, j], block, preferred_element_type=F32)
            total = term if total is None else total + term
        summed[b] = total

    first_leaves = [b for lo in range(leaves // 2) for b in (lo, lo + leaves // 2)]
    pending_near = list(range(1, leaves - 1)) + [0, leaves - 1]
    waited = set()
    stores = []
    clock = 0.0
    for when, level, slot in event_order(leaves, dev_bits):
        b = first_leaves[slot]
        while pending_near and when - clock > 0.4 and level > 0:
            near_field(pending_near.pop(0))
            clock += 0.4
        clock = max(clock, when)
        copies[level, b].wait_recv()
        q = local_bits + level
        if q not in waited:
            coup_loads[q].wait()
            waited.add(q)
        mixed = mix(q, b, cross[level, b].reshape(2 * rank, rank))
        if level + 1 < dev_bits:
            cross[level + 1, b, sides[level + 1]] = mixed
            send(level + 1, b)
            continue
        if not stores:
            basis_load.wait()
        while b in pending_near:
            near_field(pending_near.pop(0))
        far = jnp.dot(
            basis_out[pl.ds(b * rows, rows), :], mixed, preferred_element_type=F32
        )
        result[b] = (summed[b] + far).astype(BF16)
        store = pltpu.make_async_copy(
            result.at[b], result_hbm.at[pl.ds(b * rows, rows)], store_sem.at[b]
        )
        store.start()
        stores.append(store)

    for copy in copies.values():
        copy.wait_send()
    to_left.wait_send()
    to_right.wait_send()
    for store in stores:
        store.wait()


def per_device(fields, in_basis, out_basis, couplings, near_blocks):
    leaves, _, rows, _ = near_blocks.shape
    cols = fields.shape[1]
    rank = in_basis.shape[1]
    levels = couplings.shape[0]
    count = lax.axis_size("leaf")
    dev_bits = count.bit_length() - 1
    local_bits = levels - dev_bits
    dma = pltpu.SemaphoreType.DMA
    return pl.pallas_call(
        functools.partial(kernel, count),
        out_shape=jax.ShapeDtypeStruct(fields.shape, BF16),
        in_specs=[pl.BlockSpec(memory_space=pl.ANY)] * 5,
        out_specs=pl.BlockSpec(memory_space=pl.ANY),
        scratch_shapes=[
            pltpu.VMEM(((leaves + 2) * rows, cols), BF16),
            pltpu.VMEM((leaves * rows, rank), BF16),
            pltpu.VMEM((leaves * rows, rank), BF16),
            pltpu.VMEM(couplings.shape, BF16),
            pltpu.VMEM(near_blocks.shape, BF16),
            pltpu.VMEM((local_bits, leaves, rank, cols), BF16),
            pltpu.VMEM((dev_bits, leaves, 2, rank, cols), BF16),
            pltpu.VMEM((leaves, rank, cols), BF16),
            pltpu.VMEM((leaves, rows, cols), F32),
            pltpu.VMEM((leaves, rows, cols), BF16),
            dma((2, leaves // 2)),
            dma((levels,)),
            dma((leaves,)),
            dma,
            dma((leaves,)),
            dma((2,)),
            dma((2,)),
            dma((dev_bits, leaves)),
            dma((dev_bits, leaves)),
        ],
        compiler_params=pltpu.CompilerParams(
            collective_id=0, has_side_effects=True, vmem_limit_bytes=60 * 1024 * 1024
        ),
        name="butterfly",
    )(fields, in_basis, out_basis, couplings, near_blocks)


def solution(mesh):
    placed = (
        P("leaf", None),
        P("leaf", None),
        P("leaf", None),
        P(None, "leaf", None, None, None),
        P("leaf", None, None, None),
    )
    return jax.shard_map(
        per_device, mesh=mesh, in_specs=placed, out_specs=P("leaf", None), check_vma=False
    )
```

```python
import functools

import jax
import jax.numpy as jnp
from jax import lax
from jax.experimental import pallas as pl
from jax.experimental.pallas import tpu as pltpu
from jax.sharding import PartitionSpec as P

MESH = pl.DeviceIdType.MESH
F32 = jnp.float32
BF16 = jnp.bfloat16


def event_order(leaves, dev_bits):
    cost = [
        (0.9, 0.10, "c"),
        (1.7, 0.70, "x"),
        (2.4, 0.70, "x"),
        (1.7, 0.70, "z"),
        (2.4, 1.40, "z"),
        (4.0, 1.90, "z"),
        (1.7, 0.70, "y"),
        (2.4, 0.70, "y"),
    ]
    cost = [cost[level % len(cost)] for level in range(dev_bits)]
    busy = {}
    core = 0.0
    queue = []
    for leaf in range(leaves):
        core += 0.15
        start = max(core, busy.get(cost[0][2], 0.0))
        busy[cost[0][2]] = start + cost[0][1]
        queue.append((start + cost[0][1] + cost[0][0], 0, leaf))
    order = []
    while queue:
        queue.sort()
        ready, level, leaf = queue.pop(0)
        order.append((max(ready, core), level, leaf))
        core = max(ready, core) + 0.15
        if level + 1 < dev_bits:
            flight, wire, row = cost[level + 1]
            start = max(core, busy.get(row, 0.0))
            busy[row] = start + wire
            queue.append((start + wire + flight, level + 1, leaf))
    return order


def kernel(
    count,
    fields_hbm,
    in_hbm,
    out_hbm,
    coup_hbm,
    near_hbm,
    result_hbm,
    fields,
    basis_in,
    basis_out,
    coup,
    near,
    local,
    cross,
    final,
    summed,
    result,
    load_sem,
    coup_sem,
    near_sem,
    basis_sem,
    store_sem,
    halo_send,
    halo_recv,
    send_sem,
    recv_sem,
):
    leaves = near.shape[0]
    rows = near.shape[2]
    rank = basis_in.shape[1]
    levels = coup.shape[0]
    dev_bits = cross.shape[0]
    local_bits = levels - dev_bits
    me = lax.axis_index("leaf")
    right = lax.rem(me + 1, count)
    left = lax.rem(me + count - 1, count)
    sides = [lax.rem(lax.div(me, 1 << k), 2) for k in range(dev_bits)]
    partners = [me + (1 << k) * (1 - 2 * sides[k]) for k in range(dev_bits)]

    pair_rows = 2 * rows
    loads = []
    for pair in range(leaves // 2):
        at = pl.ds(pair * pair_rows, pair_rows)
        to = pl.ds(rows + pair * pair_rows, pair_rows)
        loads.append(
            (
                pltpu.make_async_copy(fields_hbm.at[at], fields.at[to], load_sem.at[0, pair]),
                pltpu.make_async_copy(in_hbm.at[at], basis_in.at[at], load_sem.at[1, pair]),
            )
        )
    coup_loads = [
        pltpu.make_async_copy(coup_hbm.at[q], coup.at[q], coup_sem.at[q]) for q in range(levels)
    ]
    near_loads = [
        pltpu.make_async_copy(near_hbm.at[b], near.at[b], near_sem.at[b]) for b in range(leaves)
    ]
    basis_load = pltpu.make_async_copy(out_hbm, basis_out, basis_sem)

    for pair in loads:
        for load in pair:
            load.start()
    for q in range(local_bits):
        coup_loads[q].start()

    barrier = pltpu.get_barrier_semaphore()
    for other in partners + [left, right]:
        pl.semaphore_signal(barrier, inc=1, device_id=(other,), device_id_type=MESH)

    for b in range(leaves):
        if b % 2 == 0:
            for load in loads[b // 2]:
                load.wait()
        local[0, b] = lax.dot_general(
            basis_in[pl.ds(b * rows, rows), :],
            fields[pl.ds((b + 1) * rows, rows), :],
            (((0,), (0,)), ((), ())),
            preferred_element_type=F32,
        ).astype(BF16)

    for q in range(local_bits, levels):
        coup_loads[q].start()
    for b in range(leaves):
        near_loads[b].start()
    basis_load.start()

    def mix(q, b, stacked):
        both = jnp.concatenate([coup[q, b, 0], coup[q, b, 1]], axis=1)
        return jnp.dot(both, stacked, preferred_element_type=F32).astype(BF16)

    copies = {}

    def send(level, b):
        copy = pltpu.make_async_remote_copy(
            src_ref=cross.at[level, b, sides[level]],
            dst_ref=cross.at[level, b, sides[level]],
            send_sem=send_sem.at[level, b],
            recv_sem=recv_sem.at[level, b],
            device_id=(partners[level],),
            device_id_type=MESH,
        )
        copy.start()
        copies[level, b] = copy

    for q in range(local_bits):
        coup_loads[q].wait()
        if q == local_bits - 1:
            pl.semaphore_wait(barrier, dev_bits + 2)
        stride = 1 << q
        for lo in range(leaves):
            if lo & stride:
                continue
            hi = lo | stride
            stacked = jnp.concatenate([local[q, lo], local[q, hi]], axis=0)
            for b in (lo, hi):
                mixed = mix(q, b, stacked)
                if q + 1 < local_bits:
                    local[q + 1, b] = mixed
                else:
                    cross[0, b, sides[0]] = mixed
                    send(0, b)

    to_left = pltpu.make_async_remote_copy(
        src_ref=fields.at[pl.ds(rows, rows)],
        dst_ref=fields.at[pl.ds((leaves + 1) * rows, rows)],
        send_sem=halo_send.at[0],
        recv_sem=halo_recv.at[0],
        device_id=(left,),
        device_id_type=MESH,
    )
    to_right = pltpu.make_async_remote_copy(
        src_ref=fields.at[pl.ds(leaves * rows, rows)],
        dst_ref=fields.at[pl.ds(0, rows)],
        send_sem=halo_send.at[1],
        recv_sem=halo_recv.at[1],
        device_id=(right,),
        device_id_type=MESH,
    )
    to_left.start()
    to_right.start()

    def near_field(b):
        near_loads[b].wait()
        if b == 0:
            to_right.wait_recv()
        if b == leaves - 1:
            to_left.wait_recv()
        total = None
        for j in range(3):
            block = fields[pl.ds((b + j) * rows, rows), :]
            if b == 0 and j == 0:
                block = jnp.where(me > 0, block, jnp.zeros_like(block))
            if b == leaves - 1 and j == 2:
                block = jnp.where(me < count - 1, block, jnp.zeros_like(block))
            term = jnp.dot(near[b, j], block, preferred_element_type=F32)
            total = term if total is None else total + term
        summed[b] = total

    first_leaves = [b for lo in range(leaves // 2) for b in (lo, lo + leaves // 2)]
    pending_near = list(range(1, leaves - 1)) + [0, leaves - 1]
    waited = set()
    stores = []
    clock = 0.0
    for when, level, slot in event_order(leaves, dev_bits):
        b = first_leaves[slot]
        while pending_near and when - clock > 0.4 and level > 0:
            near_field(pending_near.pop(0))
            clock += 0.4
        clock = max(clock, when)
        copies[level, b].wait_recv()
        q = local_bits + level
        if q not in waited:
            coup_loads[q].wait()
            waited.add(q)
        mixed = mix(q, b, cross[level, b].reshape(2 * rank, rank))
        if level + 1 < dev_bits:
            cross[level + 1, b, sides[level + 1]] = mixed
            send(level + 1, b)
            continue
        if not stores:
            basis_load.wait()
        while b in pending_near:
            near_field(pending_near.pop(0))
        far = jnp.dot(
            basis_out[pl.ds(b * rows, rows), :], mixed, preferred_element_type=F32
        )
        result[b] = (summed[b] + far).astype(BF16)
        store = pltpu.make_async_copy(
            result.at[b], result_hbm.at[pl.ds(b * rows, rows)], store_sem.at[b]
        )
        store.start()
        stores.append(store)

    for copy in copies.values():
        copy.wait_send()
    to_left.wait_send()
    to_right.wait_send()
    for store in stores:
        store.wait()


def per_device(fields, in_basis, out_basis, couplings, near_blocks):
    leaves, _, rows, _ = near_blocks.shape
    cols = fields.shape[1]
    rank = in_basis.shape[1]
    levels = couplings.shape[0]
    count = lax.axis_size("leaf")
    dev_bits = count.bit_length() - 1
    local_bits = levels - dev_bits
    dma = pltpu.SemaphoreType.DMA
    return pl.pallas_call(
        functools.partial(kernel, count),
        out_shape=jax.ShapeDtypeStruct(fields.shape, BF16),
        in_specs=[pl.BlockSpec(memory_space=pl.ANY)] * 5,
        out_specs=pl.BlockSpec(memory_space=pl.ANY),
        scratch_shapes=[
            pltpu.VMEM(((leaves + 2) * rows, cols), BF16),
            pltpu.VMEM((leaves * rows, rank), BF16),
            pltpu.VMEM((leaves * rows, rank), BF16),
            pltpu.VMEM(couplings.shape, BF16),
            pltpu.VMEM(near_blocks.shape, BF16),
            pltpu.VMEM((local_bits, leaves, rank, cols), BF16),
            pltpu.VMEM((dev_bits, leaves, 2, rank, cols), BF16),
            pltpu.VMEM((leaves, rank, cols), BF16),
            pltpu.VMEM((leaves, rows, cols), F32),
            pltpu.VMEM((leaves, rows, cols), BF16),
            dma((2, leaves // 2)),
            dma((levels,)),
            dma((leaves,)),
            dma,
            dma((leaves,)),
            dma((2,)),
            dma((2,)),
            dma((dev_bits, leaves)),
            dma((dev_bits, leaves)),
        ],
        compiler_params=pltpu.CompilerParams(
            collective_id=0, has_side_effects=True, vmem_limit_bytes=60 * 1024 * 1024
        ),
        name="butterfly",
    )(fields, in_basis, out_basis, couplings, near_blocks)


def solution(mesh):
    placed = (
        P("leaf", None),
        P("leaf", None),
        P("leaf", None),
        P(None, "leaf", None, None, None),
        P("leaf", None, None, None),
    )
    return jax.shard_map(
        per_device, mesh=mesh, in_specs=placed, out_specs=P("leaf", None), check_vma=False
    )
```
